512 devices in a mesh: seq: 64 (over z, x), head: 8 (over y, core).
Axes of the slice: x: 4, y: 4, z: 16, core: 2. Of those that a mesh axis runs over, the one named last changes fastest.
Arguments:
- hidden: bfloat16 [32768, 4096], P('seq'), may hold values from -6 to 6
- steer: bfloat16 [4096], replicated, may hold values from -4 to 4
- w_x: bfloat16 [4096, 4096], P('seq', 'head'), may hold values from -0.09375 to 0.09375
- w_z: bfloat16 [4096, 4096], P('seq', 'head'), may hold values from -0.09375 to 0.09375
- w_shared: bfloat16 [4096, 320], P(('seq', 'head')), may hold values from -0.09375 to 0.09375
- conv_x: float32 [4, 4096], P(None, 'head'), may hold values from -3 to 3
- conv_shared: float32 [4, 256], replicated, may hold values from -3 to 3
- dt_bias: float32 [64], P('head'), may hold values from -7 to 0
- decay_rate: float32 [64], P('head'), may hold values from 0.01 to 16
- skip: float32 [64], P('head'), may hold values from 0.5 to 1.5
- norm_gain: float32 [4096], P('head'), may hold values from 0.5 to 1.5
Outputs:
- mixed: bfloat16 [32768, 4096], P('seq', 'head')
The draws below stay inside these ranges and needn't reach their ends.
All inputs are finite; a program needn't handle non-finite values.
Results may differ from the reference program's by a relative error of at most 0.0095.
Values may be sent and summed in bfloat16 or wider, within the bound.
No kernel may reach another device: no remote copies, remote signals or barrier semaphores. Data moves between devices by JAX's collectives and lax.ppermute only.
A program may use at most 128 MiB of HBM per device.

```python
import math
import jax
import jax.numpy as jnp
from jax import lax

D = 4096
HEADS = 64
HEAD_DIM = 64
STATE = 128
CONV = 4
SPAN = 128
TOKENS = 32768
INNER = 4096


def steps_of(key, shape, shards, smallest, largest):
    gain = 1.0
    for axis_at, shards_of in shards:
        draws = jax.random.uniform(jax.random.fold_in(jax.random.fold_in(key, 6), axis_at), (shards_of,), jnp.float32, smallest / len(shards), largest / len(shards))
        gain = gain * jnp.repeat(jnp.exp(draws), shape[axis_at] // shards_of).reshape((-1,) + (1,) * (len(shape) - 1 - axis_at))
    return gain


def normal_values(rng, dims, deviation, reach, pieces=(), dtype=jnp.bfloat16):
    loudness = steps_of(rng, dims, pieces, -0.22, 0.18) if pieces else 1.0
    entries = jax.random.normal(rng, dims, jnp.float32) * deviation * loudness
    return jnp.minimum(jnp.maximum(entries, -reach), reach).astype(dtype)


def setup_inputs(seed: int = 0) -> dict:
    arg_keys = jax.random.split(jax.random.key(seed), 12)
    hidden = normal_values(arg_keys[0], (TOKENS, D), 1.0, 6.0, ((0, 64),))
    steer = normal_values(arg_keys[1], (D,), 1.0, 4.0)
    w_x = normal_values(arg_keys[2], (D, INNER), D ** -0.5, 0.09375, ((0, 64), (1, 8)))
    w_z = normal_values(arg_keys[3], (D, INNER), D ** -0.5, 0.09375, ((0, 64), (1, 8)))
    w_shared = normal_values(arg_keys[4], (D, 2 * STATE + HEADS), D ** -0.5, 0.09375, ((0, 512),))
    conv_x = normal_values(arg_keys[5], (CONV, INNER), CONV ** -0.5, 3.0, ((1, 8),), jnp.float32)
    conv_shared = normal_values(arg_keys[6], (CONV, 2 * STATE), CONV ** -0.5, 3.0, (), jnp.float32)
    dt_bias = jnp.clip(-7.0 + 7.0 * jax.random.uniform(arg_keys[7], (HEADS,), jnp.float32) ** steps_of(arg_keys[7], (HEADS,), ((0, 8),), -0.2, 0.2), -7.0, 0.0)
    decay_rate = jnp.clip(jnp.exp(math.log(16.0) - 7.377759 * jax.random.uniform(arg_keys[8], (HEADS,), jnp.float32) ** steps_of(arg_keys[8], (HEADS,), ((0, 8),), -0.2, 0.2)), 0.01, 16.0)
    skip = jnp.clip(0.5 + 1.0 * jax.random.uniform(arg_keys[9], (HEADS,), jnp.float32) ** steps_of(arg_keys[9], (HEADS,), ((0, 8),), -0.2, 0.2), 0.5, 1.5)
    norm_gain = jnp.clip(1.0 + 0.1 * jax.random.normal(arg_keys[10], (INNER,), jnp.float32), 0.5, 1.5)
    return dict(hidden=hidden, steer=steer, w_x=w_x, w_z=w_z, w_shared=w_shared, conv_x=conv_x, conv_shared=conv_shared, dt_bias=dt_bias, decay_rate=decay_rate, skip=skip, norm_gain=norm_gain)


highest = lax.Precision.HIGHEST

def conv_valid(extended, weights):
    taps = weights.shape[0]
    count = extended.shape[0] - taps + 1
    values = extended.astype(jnp.float32)
    total = jnp.zeros((count, extended.shape[1]), jnp.float32)
    for k in range(taps):
        total = total + values[k:k + count] * weights[k]
    return total

def span_pass(inputs, steps, logs, in_map, out_map, start):
    blocks = inputs.shape[0] // SPAN
    heads = inputs.shape[1]
    width = inputs.shape[2]
    index = jnp.arange(SPAN)
    lower = index[:, None] >= index[None, :]

    def advance(state, block):
        xblock, dblock, lblock, bblock, cblock = block
        cums = jnp.cumsum(lblock, axis=0)
        gram = jnp.dot(cblock, bblock.T, precision=highest)
        diff = cums[:, None, :] - cums[None, :, :]
        decay = jnp.exp(jnp.where(lower[:, :, None], diff, -1e+30))
        weights = gram[:, :, None] * decay * dblock[None, :, :]
        within = jnp.einsum('ijh,jhp->ihp', weights, xblock, precision=highest)
        carried = jnp.einsum('in,hpn->ihp', cblock, state, precision=highest) * jnp.exp(cums)[:, :, None]
        tail = jnp.exp(cums[-1][None, :] - cums) * dblock
        fresh = jnp.einsum('jh,jhp,jn->hpn', tail, xblock, bblock, precision=highest)
        state = jnp.exp(cums[-1])[:, None, None] * state + fresh
        return (state, within + carried)
    final, outs = lax.scan(advance, start, (inputs.reshape(blocks, SPAN, heads, width), steps.reshape(blocks, SPAN, heads), logs.reshape(blocks, SPAN, heads), in_map.reshape(blocks, SPAN, in_map.shape[1]), out_map.reshape(blocks, SPAN, out_map.shape[1])))
    return (outs.reshape(-1, heads, width), final)

def reference(hidden, steer, w_x, w_z, w_shared, conv_x, conv_shared, dt_bias, decay_rate, skip, norm_gain):
    count = hidden.shape[0]
    steered = (hidden.astype(jnp.float32) + steer.astype(jnp.float32)).astype(jnp.bfloat16)
    x_raw = jnp.dot(steered, w_x, preferred_element_type=jnp.float32).astype(jnp.bfloat16)
    z_raw = jnp.dot(steered, w_z, preferred_element_type=jnp.float32).astype(jnp.bfloat16)
    shared = jnp.dot(steered, w_shared, preferred_element_type=jnp.float32)
    b_raw = shared[:, :2 * STATE].astype(jnp.bfloat16)
    dt_raw = shared[:, 2 * STATE:]
    x_pad = jnp.concatenate([jnp.zeros((CONV - 1, x_raw.shape[1]), jnp.bfloat16), x_raw], axis=0)
    b_pad = jnp.concatenate([jnp.zeros((CONV - 1, b_raw.shape[1]), jnp.bfloat16), b_raw], axis=0)
    x_conv = jax.nn.silu(conv_valid(x_pad, conv_x)).astype(jnp.bfloat16)
    b_conv = jax.nn.silu(conv_valid(b_pad, conv_shared)).astype(jnp.bfloat16)
    in_map = b_conv[:, :STATE].astype(jnp.float32)
    out_map = b_conv[:, STATE:].astype(jnp.float32)
    steps = jax.nn.softplus(dt_raw + dt_bias)
    logs = -steps * decay_rate
    inputs = x_conv.astype(jnp.float32).reshape(count, HEADS, HEAD_DIM)
    start = jnp.zeros((HEADS, HEAD_DIM, STATE), jnp.float32)
    heads_out, final = span_pass(inputs, steps, logs, in_map, out_map, start)
    heads_out = heads_out + skip[None, :, None] * inputs
    gated = heads_out.reshape(count, HEADS * HEAD_DIM) * jax.nn.silu(z_raw.astype(jnp.float32))
    scale = lax.rsqrt(lax.optimization_barrier(jnp.mean(gated * gated, axis=1, keepdims=True)) + 1e-05)
    return (gated * scale * norm_gain).astype(jnp.bfloat16)
```

```python
import jax
import jax.numpy as jnp
from jax import lax
from jax.experimental import pallas as pl
from jax.experimental.pallas import tpu as pltpu
from jax.sharding import Mesh, PartitionSpec as P

STATE = 128
CONV = 4
SPAN = 128
HALO = 16
DIM = 64
LOGS = 16

SEQ = ("zh", "zl", "x")
HEAD = ("y", "c")
SIZES = {"zh": 4, "zl": 4, "x": 4, "y": 4, "c": 2}


f32 = jnp.float32
bf16 = jnp.bfloat16
exact = lax.Precision.HIGHEST


def size_of(axes):
    n = 1
    for a in (axes,) if isinstance(axes, str) else axes:
        n *= SIZES[a]
    return n


def shifted(block, axis, by, wrap=True):
    n = size_of(axis)
    route = [(i, (i + by) % n) for i in range(n) if wrap or 0 <= i + by < n]
    return lax.ppermute(block, axis, route)


def spread(block, axis):
    n = size_of(axis)
    return lax.all_to_all(jnp.broadcast_to(block[None], (n,) + block.shape), axis, 0, 0)


def dot(a, b, dims=((1,), (0,)), precision=None):
    return lax.dot_general(a, b, (dims, ((), ())), precision=precision, preferred_element_type=f32)


def local_pass(x_ref, bc_ref, dt_ref, taps_ref, bias_ref, rate_ref, skip_ref,
               y_ref, c_ref, e_ref, s_ref):
    heads = dt_ref.shape[0]
    rows, width = y_ref.shape
    steps_t = jax.nn.softplus(dt_ref[...] + bias_ref[...])
    logs_t = -steps_t * rate_ref[...]
    r = lax.broadcasted_iota(jnp.int32, (SPAN, SPAN), 0)
    c = lax.broadcasted_iota(jnp.int32, (SPAN, SPAN), 1)
    lower = r >= c
    tril = lower.astype(f32)
    eye = (r == c).astype(f32)
    spot = (
        lax.broadcasted_iota(jnp.int32, (heads, width), 1) // DIM
        == lax.broadcasted_iota(jnp.int32, (heads, width), 0)
    ).astype(f32)
    taps = taps_ref[...]
    skip = skip_ref[...]
    state = jnp.zeros((STATE, width), f32)
    before = jnp.ones((1, width), f32)
    total = jnp.zeros((1, width), f32)
    for k in range(rows // SPAN):
        at = k * SPAN
        ext = x_ref[at : at + SPAN + HALO, :].astype(f32)
        conv = jnp.zeros((SPAN, width), f32)
        for j in range(CONV):
            first = HALO - CONV + 1 + j
            conv = conv + ext[first : first + SPAN] * taps[j : j + 1, :]
        xb = (conv * jax.nn.sigmoid(conv)).astype(bf16)
        xf = xb.astype(f32)
        bt = bc_ref[:STATE, at : at + SPAN]
        cm = bc_ref[STATE:, at : at + SPAN].astype(f32).T.astype(bf16)
        c_ref[at : at + SPAN, :] = cm
        lt = logs_t[:, at : at + SPAN]
        st = steps_t[:, at : at + SPAN]
        cum_t = dot(lt, tril, ((1,), (1,)), exact)
        cum = dot(tril, lt, ((1,), (1,)), exact)
        step = dot(eye, st, ((1,), (1,)), exact)
        gram = dot(cm, bt)
        inside = []
        for h in range(heads):
            diff = cum[:, h : h + 1] - cum_t[h : h + 1, :]
            decay = jnp.exp(jnp.where(lower, diff, -1e30))
            weights = gram * decay * st[h : h + 1, :]
            inside.append(dot(weights.astype(bf16), xb[:, h * DIM : (h + 1) * DIM]))
        within = jnp.concatenate(inside, axis=1)
        last = cum[SPAN - 1 :, :]
        grown = dot(jnp.exp(cum), spot, precision=exact)
        tail = dot(jnp.exp(last - cum) * step, spot, precision=exact)
        carried = dot(cm, state.astype(bf16)) * grown
        fresh = dot(bt, (tail * xf).astype(bf16))
        end = grown[SPAN - 1 :, :]
        state = end * state + fresh
        y_ref[at : at + SPAN, :] = within + carried + skip * xf
        e_ref[at : at + SPAN, :] = grown * before
        before = before * end
        total = total + dot(last, spot, precision=exact)
    high = total.astype(bf16)
    low = (total - high.astype(f32)).astype(bf16)
    row = lax.broadcasted_iota(jnp.int32, (LOGS, STATE), 0)
    for g in range(width // STATE):
        lanes = slice(g * STATE, (g + 1) * STATE)
        s_ref[g, :STATE, :] = state[:, lanes].astype(bf16)
        both = jnp.where(row == 0, high[:, lanes].astype(f32), 0.0)
        both = jnp.where(row == 1, low[:, lanes].astype(f32), both)
        s_ref[g, STATE:, :] = both.astype(bf16)


def piece(ref, k):
    logs = ref[k, STATE:, :].astype(f32)
    return ref[k, :STATE, :].astype(f32), logs[0:1] + logs[1:2]


def group_pass(r_ref, o_ref):
    state, log = piece(r_ref, 0)
    for k in range(1, r_ref.shape[0]):
        here, more = piece(r_ref, k)
        state = jnp.exp(more) * state + here
        log = log + more
    o_ref[:STATE, :] = state.astype(bf16)
    high = log.astype(bf16).astype(f32)
    row = lax.broadcasted_iota(jnp.int32, (LOGS, STATE), 0)
    both = jnp.where(row == 0, high, jnp.where(row == 1, log - high, 0.0))
    o_ref[STATE:, :] = both.astype(bf16)


def prefix_pass(at_ref, t_ref, r_ref, o_ref):
    state = jnp.zeros((STATE, STATE), f32)
    for k in range(t_ref.shape[0]):
        here, log = piece(t_ref, k)
        state = jnp.where(k < at_ref[0], jnp.exp(log) * state + here, state)
    for k in range(r_ref.shape[0]):
        o_ref[k] = state.astype(bf16)
        here, log = piece(r_ref, k)
        state = jnp.exp(log) * state + here


def gate_pass(y_ref, c_ref, e_ref, s_ref, z_ref, g_ref, q_ref):
    rows, width = y_ref.shape
    ones = jnp.ones((8, STATE), f32)
    for k in range(rows // SPAN):
        at = slice(k * SPAN, (k + 1) * SPAN)
        cm = c_ref[at, :]
        squares = jnp.zeros((SPAN, STATE), f32)
        for g in range(width // STATE):
            lanes = slice(g * STATE, (g + 1) * STATE)
            z = z_ref[at, lanes].astype(f32)
            y = y_ref[at, lanes] + dot(cm, s_ref[g]) * e_ref[at, lanes]
            gated = y * (z * jax.nn.sigmoid(z))
            g_ref[at, lanes] = gated
            squares = squares + gated * gated
        q_ref[:, at] = dot(ones, squares, ((1,), (1,)), exact)


def call(kernel, outs, *args, scalars=0):
    vmem = pl.BlockSpec(memory_space=pltpu.VMEM)
    smem = pl.BlockSpec(memory_space=pltpu.SMEM)
    return pl.pallas_call(
        kernel,
        out_shape=outs,
        in_specs=[smem] * scalars + [vmem] * (len(args) - scalars),
        out_specs=jax.tree.map(lambda _: vmem, outs),
        name=kernel.__name__,
        cost_estimate=pl.CostEstimate(flops=10**9, bytes_accessed=4 * 10**6, transcendentals=10**6),
    )(*args)


def shape(dims, kind):
    return jax.ShapeDtypeStruct(dims, kind)


def gather_x(w):
    half = w.shape[0] // 2
    left, right = shifted(w, "x", 1), shifted(w, "x", -1)
    far_a, far_b = shifted(left[:half], "x", 1), shifted(right[half:], "x", -1)
    return ((0, w), (-1, left), (1, right), (2, jnp.concatenate([far_a, far_b], axis=0)))


def on_device(
    hidden, steer, w_x, w_z, w_shared, conv_x, conv_shared, dt_bias, decay_rate, skip, norm_gain
):
    rows = hidden.shape[0]
    heads = dt_bias.shape[0]
    width = w_x.shape[1]
    ways = size_of(HEAD)
    maps = 2 * STATE // ways
    head_at = lax.axis_index(HEAD)
    seq_at = lax.axis_index(SEQ)
    x_at = lax.axis_index("x")
    z_at = lax.axis_index(("zh", "zl"))

    z_full = lax.all_gather(w_z, SEQ, axis=0, tiled=True)

    halo = shifted(hidden[rows - HALO :], SEQ, 1, wrap=False)
    ext = jnp.concatenate([halo, hidden], axis=0)
    ext = (ext.astype(f32) + steer.astype(f32)).astype(bf16)
    k = hidden.shape[1]
    per = k // size_of(SEQ)
    turned = ext.reshape(-1, 4, 4, 4, per).transpose(0, 3, 2, 1, 4).reshape(-1, k)

    small = w_shared.shape[0]
    share = jnp.concatenate(
        [
            w_shared[:, : 2 * STATE].reshape(small, ways, maps),
            w_shared[:, 2 * STATE :].reshape(small, ways, heads),
        ],
        axis=2,
    ).transpose(1, 0, 2)
    share = lax.all_to_all(share, HEAD, 0, 0).reshape(ways * small, maps + heads)
    w = jnp.concatenate([w_x, share], axis=1)
    w = spread(w, "zh").reshape(-1, w.shape[1])
    w = spread(w, "zl").reshape(-1, w.shape[1])
    x_sum = jnp.zeros((rows + HALO, width), f32)
    s_sum = jnp.zeros((maps + heads, rows + HALO), f32)
    depth = w.shape[0]
    for offset, block in gather_x(w):
        start = lax.rem(x_at + (offset + 4), 4) * depth
        columns = lax.dynamic_slice_in_dim(turned, start, depth, 1)
        x_sum = x_sum + dot(columns, block[:, :width])
        s_sum = s_sum + dot(block[:, width:], columns, ((0,), (1,)))

    early = (lax.broadcasted_iota(jnp.int32, (rows + HALO, 1), 0) < HALO) & (seq_at == 0)
    x_raw = jnp.where(early, 0.0, x_sum).astype(bf16)
    b_raw = jnp.where(early.reshape(1, -1), 0.0, s_sum[:maps]).astype(bf16).astype(f32)
    taps = lax.dynamic_slice_in_dim(conv_shared, head_at * maps, maps, 1).T
    b_conv = jnp.zeros((maps, rows), f32)
    for j in range(CONV):
        first = HALO - CONV + 1 + j
        b_conv = b_conv + b_raw[:, first : first + rows] * taps[:, j : j + 1]
    b_conv = jax.nn.silu(b_conv).astype(bf16)
    both = spread(b_conv, HEAD).reshape(2 * STATE, rows)

    groups = width // STATE
    y, c_map, grown, ends = call(
        local_pass,
        (
            shape((rows, width), f32),
            shape((rows, STATE), bf16),
            shape((rows, width), f32),
            shape((groups, STATE + LOGS, STATE), bf16),
        ),
        x_raw,
        both,
        s_sum[maps:, HALO:],
        conv_x,
        dt_bias.reshape(-1, 1),
        decay_rate.reshape(-1, 1),
        jnp.repeat(skip, DIM).reshape(1, -1),
    )

    ends = lax.all_to_all(ends, "x", 0, 0)
    mine = call(group_pass, shape((STATE + LOGS, STATE), bf16), ends)
    totals = spread(mine, ("zh", "zl"))
    starts = call(
        prefix_pass, shape((4, STATE, STATE), bf16), z_at.reshape(1), totals, ends, scalars=1
    )
    state_in = lax.all_to_all(starts, "x", 0, 0)

    z_raw = dot(ext[HALO:], z_full).astype(bf16)
    gated, squares = call(
        gate_pass,
        (shape((rows, width), f32), shape((8, rows), f32)),
        y,
        c_map,
        grown,
        state_in,
        z_raw,
    )
    squares = jnp.sum(spread(squares[0].reshape(4, -1), HEAD), axis=0).reshape(rows)
    scale = lax.rsqrt(squares / (width * ways) + 1e-05)
    return (gated * scale[:, None] * norm_gain).astype(bf16)


def solution(mesh):
    mesh = Mesh(mesh.devices.reshape(tuple(SIZES.values())), tuple(SIZES))
    placed = (
        P(SEQ, None),
        P(),
        P(SEQ, HEAD),
        P(SEQ, HEAD),
        P(SEQ + HEAD, None),
        P(None, HEAD),
        P(),
        P(HEAD),
        P(HEAD),
        P(HEAD),
        P(HEAD),
    )
    return jax.shard_map(
        on_device, mesh=mesh, in_specs=placed, out_specs=P(SEQ, HEAD), check_vma=False
    )
```

```python
import jax
import jax.numpy as jnp
from jax import lax
from jax.experimental import pallas as pl
from jax.experimental.pallas import tpu as pltpu
from jax.sharding import Mesh, PartitionSpec as P

STATE = 128
CONV = 4
SPAN = 128
HALO = 16
DIM = 64
LOGS = 16

SEQ = ("zh", "zl", "x")
HEAD = ("y", "c")
Z = ("zh", "zl")
SIZES = {"zh": 4, "zl": 4, "x": 4, "y": 4, "c": 2}


f32 = jnp.float32
bf16 = jnp.bfloat16
exact = lax.Precision.HIGHEST


def size_of(axes):
    n = 1
    for a in (axes,) if isinstance(axes, str) else axes:
        n *= SIZES[a]
    return n


def shifted(block, axis, by, wrap=True):
    n = size_of(axis)
    route = [(i, (i + by) % n) for i in range(n) if wrap or 0 <= i + by < n]
    return lax.ppermute(block, axis, route)


def spread(block, axis):
    n = size_of(axis)
    return lax.all_to_all(jnp.broadcast_to(block[None], (n,) + block.shape), axis, 0, 0)


def dot(a, b, dims=((1,), (0,)), precision=None):
    return lax.dot_general(a, b, (dims, ((), ())), precision=precision, preferred_element_type=f32)


def local_pass(x_ref, bc_ref, dt_ref, taps_ref, bias_ref, rate_ref, skip_ref,
               y_ref, c_ref, e_ref, s_ref):
    heads = dt_ref.shape[0]
    rows, width = y_ref.shape
    steps_t = jax.nn.softplus(dt_ref[...] + bias_ref[...])
    logs_t = -steps_t * rate_ref[...]
    r = lax.broadcasted_iota(jnp.int32, (SPAN, SPAN), 0)
    c = lax.broadcasted_iota(jnp.int32, (SPAN, SPAN), 1)
    lower = r >= c
    tril = lower.astype(f32)
    eye = (r == c).astype(f32)
    spot = (
        lax.broadcasted_iota(jnp.int32, (heads, width), 1) // DIM
        == lax.broadcasted_iota(jnp.int32, (heads, width), 0)
    ).astype(f32)
    taps = taps_ref[...]
    skip = skip_ref[...]
    state = jnp.zeros((STATE, width), f32)
    before = jnp.ones((1, width), f32)
    total = jnp.zeros((1, width), f32)
    for k in range(rows // SPAN):
        at = k * SPAN
        ext = x_ref[at : at + SPAN + HALO, :].astype(f32)
        conv = jnp.zeros((SPAN, width), f32)
        for j in range(CONV):
            first = HALO - CONV + 1 + j
            conv = conv + ext[first : first + SPAN] * taps[j : j + 1, :]
        xb = (conv * jax.nn.sigmoid(conv)).astype(bf16)
        xf = xb.astype(f32)
        bt = bc_ref[:STATE, at : at + SPAN]
        cm = bc_ref[STATE:, at : at + SPAN].astype(f32).T.astype(bf16)
        c_ref[at : at + SPAN, :] = cm
        lt = logs_t[:, at : at + SPAN]
        st = steps_t[:, at : at + SPAN]
        cum_t = dot(lt, tril, ((1,), (1,)), exact)
        cum = dot(tril, lt, ((1,), (1,)), exact)
        step = dot(eye, st, ((1,), (1,)), exact)
        gram = dot(cm, bt)
        inside = []
        for h in range(heads):
            diff = cum[:, h : h + 1] - cum_t[h : h + 1, :]
            decay = jnp.exp(jnp.where(lower, diff, -1e30))
            weights = gram * decay * st[h : h + 1, :]
            inside.append(dot(weights.astype(bf16), xb[:, h * DIM : (h + 1) * DIM]))
        within = jnp.concatenate(inside, axis=1)
        last = cum[SPAN - 1 :, :]
        grown = dot(jnp.exp(cum), spot, precision=exact)
        tail = dot(jnp.exp(last - cum) * step, spot, precision=exact)
        carried = dot(cm, state.astype(bf16)) * grown
        fresh = dot(bt, (tail * xf).astype(bf16))
        end = grown[SPAN - 1 :, :]
        state = end * state + fresh
        y_ref[at : at + SPAN, :] = within + carried + skip * xf
        e_ref[at : at + SPAN, :] = grown * before
        before = before * end
        total = total + dot(last, spot, precision=exact)
    high = total.astype(bf16)
    low = (total - high.astype(f32)).astype(bf16)
    row = lax.broadcasted_iota(jnp.int32, (LOGS, STATE), 0)
    for g in range(width // STATE):
        lanes = slice(g * STATE, (g + 1) * STATE)
        s_ref[g, :STATE, :] = state[:, lanes].astype(bf16)
        both = jnp.where(row == 0, high[:, lanes].astype(f32), 0.0)
        both = jnp.where(row == 1, low[:, lanes].astype(f32), both)
        s_ref[g, STATE:, :] = both.astype(bf16)


def piece(ref, k):
    logs = ref[k, STATE:, :].astype(f32)
    return ref[k, :STATE, :].astype(f32), logs[0:1] + logs[1:2]


def group_pass(r_ref, o_ref):
    state, log = piece(r_ref, 0)
    for k in range(1, r_ref.shape[0]):
        here, more = piece(r_ref, k)
        state = jnp.exp(more) * state + here
        log = log + more
    o_ref[:STATE, :] = state.astype(bf16)
    high = log.astype(bf16).astype(f32)
    row = lax.broadcasted_iota(jnp.int32, (LOGS, STATE), 0)
    both = jnp.where(row == 0, high, jnp.where(row == 1, log - high, 0.0))
    o_ref[STATE:, :] = both.astype(bf16)


def prefix_pass(at_ref, t_ref, r_ref, o_ref):
    state = jnp.zeros((STATE, STATE), f32)
    for k in range(t_ref.shape[0]):
        here, log = piece(t_ref, k)
        state = jnp.where(k < at_ref[0], jnp.exp(log) * state + here, state)
    for k in range(r_ref.shape[0]):
        o_ref[k] = state.astype(bf16)
        here, log = piece(r_ref, k)
        state = jnp.exp(log) * state + here


def gate_pass(y_ref, c_ref, e_ref, s_ref, z_ref, g_ref, q_ref):
    rows, width = y_ref.shape
    ones = jnp.ones((8, STATE), f32)
    for k in range(rows // SPAN):
        at = slice(k * SPAN, (k + 1) * SPAN)
        cm = c_ref[at, :]
        squares = jnp.zeros((SPAN, STATE), f32)
        for g in range(width // STATE):
            lanes = slice(g * STATE, (g + 1) * STATE)
            z = z_ref[at, lanes].astype(f32)
            y = y_ref[at, lanes] + dot(cm, s_ref[g]) * e_ref[at, lanes]
            gated = y * (z * jax.nn.sigmoid(z))
            g_ref[at, lanes] = gated
            squares = squares + gated * gated
        q_ref[:, at] = dot(ones, squares, ((1,), (1,)), exact)


def call(kernel, outs, *args, scalars=0):
    vmem = pl.BlockSpec(memory_space=pltpu.VMEM)
    smem = pl.BlockSpec(memory_space=pltpu.SMEM)
    return pl.pallas_call(
        kernel,
        out_shape=outs,
        in_specs=[smem] * scalars + [vmem] * (len(args) - scalars),
        out_specs=jax.tree.map(lambda _: vmem, outs),
        name=kernel.__name__,
        cost_estimate=pl.CostEstimate(flops=6 * 10**9, bytes_accessed=4 * 10**6, transcendentals=10**6),
    )(*args)


def shape(dims, kind):
    return jax.ShapeDtypeStruct(dims, kind)


def ordered(pieces, at):
    whole = jnp.zeros((4,) + pieces[0][1].shape, pieces[0][1].dtype)
    for offset, block in pieces:
        whole = lax.dynamic_update_slice(whole, block[None], (lax.rem(at + offset + 4, 4), 0, 0))
    return whole.reshape((-1,) + whole.shape[2:])


def gather_far(w, at):
    return ordered([(0, w)] + [(-d, shifted(w, Z, 4 * d)) for d in (1, -1, 2)], at)


def gather_near(w, at):
    half = w.shape[0] // 2
    two = jnp.concatenate([shifted(w[:half], Z, 2), shifted(w[half:], Z, -2)], axis=0)
    return ordered([(0, w), (-1, shifted(w, Z, 1)), (1, shifted(w, Z, -1)), (2, two)], at)


def beside(w):
    return shifted(w, "x", 1), shifted(w, "x", -1)


def opposite(left, right):
    half = left.shape[0] // 2
    a, b = shifted(left[:half], "x", 1), shifted(right[half:], "x", -1)
    return jnp.concatenate([a, b], axis=0)


def after(value, earlier):
    return lax.optimization_barrier((value, earlier))[0]


def on_device(
    hidden, steer, w_x, w_z, w_shared, conv_x, conv_shared, dt_bias, decay_rate, skip, norm_gain
):
    rows = hidden.shape[0]
    heads = dt_bias.shape[0]
    width = w_x.shape[1]
    ways = size_of(HEAD)
    maps = 2 * STATE // ways
    head_at = lax.axis_index(HEAD)
    seq_at = lax.axis_index(SEQ)
    x_at = lax.axis_index("x")
    z_at = lax.axis_index(Z)
    far_at, near_at = lax.axis_index("zh"), lax.axis_index("zl")

    halo = shifted(hidden[rows - HALO :], SEQ, 1, wrap=False)
    ext = jnp.concatenate([halo, hidden], axis=0)
    ext = (ext.astype(f32) + steer.astype(f32)).astype(bf16)
    k = hidden.shape[1]
    per = k // size_of(SEQ)
    turned = ext.reshape(-1, 4, 4, 4, per).transpose(0, 3, 2, 1, 4).reshape(-1, k)

    small = w_shared.shape[0]
    share = jnp.concatenate(
        [
            w_shared[:, : 2 * STATE].reshape(small, ways, maps),
            w_shared[:, 2 * STATE :].reshape(small, ways, heads),
        ],
        axis=2,
    ).transpose(1, 0, 2)
    share = lax.all_to_all(share, HEAD, 0, 0).reshape(ways * small, maps + heads)
    share = spread(share, "zh").reshape(-1, share.shape[1])
    share = spread(share, "zl").reshape(-1, share.shape[1])
    share = spread(share, "x").reshape(-1, share.shape[1])
    s_sum = dot(share, turned, ((0,), (1,)))

    far = gather_far(jnp.concatenate([w_x, w_z], axis=1), far_at)
    own = gather_near(far[:, :width], near_at)
    own_z = gather_near(after(far[:, width:], own), near_at)
    left, right = beside(own)
    beyond = opposite(*after((left, right), share))

    early = (lax.broadcasted_iota(jnp.int32, (rows + HALO, 1), 0) < HALO) & (seq_at == 0)
    b_raw = jnp.where(early.reshape(1, -1), 0.0, s_sum[:maps]).astype(bf16).astype(f32)
    taps = lax.dynamic_slice_in_dim(conv_shared, head_at * maps, maps, 1).T
    b_conv = jnp.zeros((maps, rows), f32)
    for j in range(CONV):
        first = HALO - CONV + 1 + j
        b_conv = b_conv + b_raw[:, first : first + rows] * taps[:, j : j + 1]
    b_conv = jax.nn.silu(b_conv).astype(bf16)
    both = spread(b_conv, HEAD).reshape(2 * STATE, rows)

    def columns_of(offset):
        depth = own.shape[0]
        return lax.dynamic_slice_in_dim(turned, lax.rem(x_at + (offset + 4), 4) * depth, depth, 1)

    x_sum = dot(columns_of(0), own) + dot(columns_of(-1), left) + dot(columns_of(1), right)
    x_sum = x_sum + dot(columns_of(2), after(beyond, (both, own_z)))
    x_raw = jnp.where(early, 0.0, x_sum).astype(bf16)
    left_z, right_z = beside(after(own_z, beyond))

    groups = width // STATE
    y, c_map, grown, ends = call(
        local_pass,
        (
            shape((rows, width), f32),
            shape((rows, STATE), bf16),
            shape((rows, width), f32),
            shape((groups, STATE + LOGS, STATE), bf16),
        ),
        x_raw,
        both,
        s_sum[maps:, HALO:],
        conv_x,
        dt_bias.reshape(-1, 1),
        decay_rate.reshape(-1, 1),
        jnp.repeat(skip, DIM).reshape(1, -1),
    )

    ends = lax.all_to_all(after(ends, (left_z, right_z)), "x", 0, 0)
    beyond_z = opposite(left_z, right_z)
    mine = call(group_pass, shape((STATE + LOGS, STATE), bf16), ends)
    totals = spread(mine, Z)
    starts = call(
        prefix_pass, shape((4, STATE, STATE), bf16), z_at.reshape(1), totals, ends, scalars=1
    )
    state_in = lax.all_to_all(starts, "x", 0, 0)

    z_sum = dot(columns_of(0)[HALO:], own_z) + dot(columns_of(-1)[HALO:], left_z)
    z_sum = z_sum + dot(columns_of(1)[HALO:], right_z) + dot(columns_of(2)[HALO:], beyond_z)
    z_raw = z_sum.astype(bf16)
    gated, squares = call(
        gate_pass,
        (shape((rows, width), f32), shape((8, rows), f32)),
        y,
        c_map,
        grown,
        state_in,
        z_raw,
    )
    squares = jnp.sum(spread(squares[0].reshape(4, -1), HEAD), axis=0).reshape(rows)
    scale = lax.rsqrt(squares / (width * ways) + 1e-05)
    return (gated * scale[:, None] * norm_gain).astype(bf16)


def solution(mesh):
    mesh = Mesh(mesh.devices.reshape(tuple(SIZES.values())), tuple(SIZES))
    placed = (
        P(SEQ, None),
        P(),
        P(SEQ, HEAD),
        P(SEQ, HEAD),
        P(SEQ + HEAD, None),
        P(None, HEAD),
        P(),
        P(HEAD),
        P(HEAD),
        P(HEAD),
        P(HEAD),
    )
    return jax.shard_map(
        on_device, mesh=mesh, in_specs=placed, out_specs=P(SEQ, HEAD), check_vma=False
    )
```

```python
import jax
import jax.numpy as jnp
from jax import lax
from jax.experimental import pallas as pl
from jax.experimental.pallas import tpu as pltpu
from jax.sharding import Mesh, PartitionSpec as P

STATE = 128
CONV = 4
SPAN = 128
HALO = 16
DIM = 64
LOGS = 16

SEQ = ("zh", "zl", "x")
HEAD = ("y", "c")
Z = ("zh", "zl")
SIZES = {"zh": 4, "zl": 4, "x": 4, "y": 4, "c": 2}


f32 = jnp.float32
bf16 = jnp.bfloat16
exact = lax.Precision.HIGHEST


def size_of(axes):
    n = 1
    for a in (axes,) if isinstance(axes, str) else axes:
        n *= SIZES[a]
    return n


def shifted(block, axis, by, wrap=True):
    n = size_of(axis)
    route = [(i, (i + by) % n) for i in range(n) if wrap or 0 <= i + by < n]
    return lax.ppermute(block, axis, route)


def spread(block, axis):
    n = size_of(axis)
    return lax.all_to_all(jnp.broadcast_to(block[None], (n,) + block.shape), axis, 0, 0)


def dot(a, b, dims=((1,), (0,)), precision=None):
    return lax.dot_general(a, b, (dims, ((), ())), precision=precision, preferred_element_type=f32)


def local_pass(x_ref, bc_ref, dt_ref, taps_ref, bias_ref, rate_ref, skip_ref,
               y_ref, c_ref, e_ref, s_ref):
    heads = dt_ref.shape[0]
    rows, width = y_ref.shape
    steps_t = jax.nn.softplus(dt_ref[...] + bias_ref[...])
    logs_t = -steps_t * rate_ref[...]
    r = lax.broadcasted_iota(jnp.int32, (SPAN, SPAN), 0)
    c = lax.broadcasted_iota(jnp.int32, (SPAN, SPAN), 1)
    lower = r >= c
    tril = lower.astype(f32)
    eye = (r == c).astype(f32)
    spot = (
        lax.broadcasted_iota(jnp.int32, (heads, width), 1) // DIM
        == lax.broadcasted_iota(jnp.int32, (heads, width), 0)
    ).astype(f32)
    taps = taps_ref[...]
    skip = skip_ref[...]
    state = jnp.zeros((STATE, width), f32)
    before = jnp.ones((1, width), f32)
    total = jnp.zeros((1, width), f32)
    for k in range(rows // SPAN):
        at = k * SPAN
        ext = x_ref[at : at + SPAN + HALO, :].astype(f32)
        conv = jnp.zeros((SPAN, width), f32)
        for j in range(CONV):
            first = HALO - CONV + 1 + j
            conv = conv + ext[first : first + SPAN] * taps[j : j + 1, :]
        xb = (conv * jax.nn.sigmoid(conv)).astype(bf16)
        xf = xb.astype(f32)
        bt = bc_ref[:STATE, at : at + SPAN]
        cm = bc_ref[STATE:, at : at + SPAN].astype(f32).T.astype(bf16)
        c_ref[at : at + SPAN, :] = cm
        lt = logs_t[:, at : at + SPAN]
        st = steps_t[:, at : at + SPAN]
        cum_t = dot(lt, tril, ((1,), (1,)), exact)
        cum = dot(tril, lt, ((1,), (1,)), exact)
        step = dot(eye, st, ((1,), (1,)), exact)
        gram = dot(cm, bt)
        inside = []
        for h in range(heads):
            diff = cum[:, h : h + 1] - cum_t[h : h + 1, :]
            decay = jnp.exp(jnp.where(lower, diff, -1e30))
            weights = gram * decay * st[h : h + 1, :]
            inside.append(dot(weights.astype(bf16), xb[:, h * DIM : (h + 1) * DIM]))
        within = jnp.concatenate(inside, axis=1)
        last = cum[SPAN - 1 :, :]
        grown = dot(jnp.exp(cum), spot, precision=exact)
        tail = dot(jnp.exp(last - cum) * step, spot, precision=exact)
        carried = dot(cm, state.astype(bf16)) * grown
        fresh = dot(bt, (tail * xf).astype(bf16))
        end = grown[SPAN - 1 :, :]
        state = end * state + fresh
        y_ref[at : at + SPAN, :] = within + carried + skip * xf
        e_ref[at : at + SPAN, :] = grown * before
        before = before * end
        total = total + dot(last, spot, precision=exact)
    high = total.astype(bf16)
    low = (total - high.astype(f32)).astype(bf16)
    row = lax.broadcasted_iota(jnp.int32, (LOGS, STATE), 0)
    for g in range(width // STATE):
        lanes = slice(g * STATE, (g + 1) * STATE)
        s_ref[g, :STATE, :] = state[:, lanes].astype(bf16)
        both = jnp.where(row == 0, high[:, lanes].astype(f32), 0.0)
        both = jnp.where(row == 1, low[:, lanes].astype(f32), both)
        s_ref[g, STATE:, :] = both.astype(bf16)


def piece(ref, k):
    logs = ref[k, STATE:, :].astype(f32)
    return ref[k, :STATE, :].astype(f32), logs[0:1] + logs[1:2]


def group_pass(r_ref, o_ref):
    state, log = piece(r_ref, 0)
    for k in range(1, r_ref.shape[0]):
        here, more = piece(r_ref, k)
        state = jnp.exp(more) * state + here
        log = log + more
    o_ref[:STATE, :] = state.astype(bf16)
    high = log.astype(bf16).astype(f32)
    row = lax.broadcasted_iota(jnp.int32, (LOGS, STATE), 0)
    both = jnp.where(row == 0, high, jnp.where(row == 1, log - high, 0.0))
    o_ref[STATE:, :] = both.astype(bf16)


def prefix_pass(at_ref, t_ref, r_ref, o_ref):
    state = jnp.zeros((STATE, STATE), f32)
    for k in range(t_ref.shape[0]):
        here, log = piece(t_ref, k)
        state = jnp.where(k < at_ref[0], jnp.exp(log) * state + here, state)
    for k in range(r_ref.shape[0]):
        o_ref[k] = state.astype(bf16)
        here, log = piece(r_ref, k)
        state = jnp.exp(log) * state + here


def gate_pass(y_ref, c_ref, e_ref, s_ref, z_ref, g_ref, q_ref):
    rows, width = y_ref.shape
    ones = jnp.ones((8, STATE), f32)
    for k in range(rows // SPAN):
        at = slice(k * SPAN, (k + 1) * SPAN)
        cm = c_ref[at, :]
        squares = jnp.zeros((SPAN, STATE), f32)
        for g in range(width // STATE):
            lanes = slice(g * STATE, (g + 1) * STATE)
            z = z_ref[at, lanes].astype(f32)
            y = y_ref[at, lanes] + dot(cm, s_ref[g]) * e_ref[at, lanes]
            gated = y * (z * jax.nn.sigmoid(z))
            g_ref[at, lanes] = gated
            squares = squares + gated * gated
        q_ref[:, at] = dot(ones, squares, ((1,), (1,)), exact)


def call(kernel, outs, *args, scalars=0):
    vmem = pl.BlockSpec(memory_space=pltpu.VMEM)
    smem = pl.BlockSpec(memory_space=pltpu.SMEM)
    return pl.pallas_call(
        kernel,
        out_shape=outs,
        in_specs=[smem] * scalars + [vmem] * (len(args) - scalars),
        out_specs=jax.tree.map(lambda _: vmem, outs),
        name=kernel.__name__,
        cost_estimate=pl.CostEstimate(flops=6 * 10**9, bytes_accessed=4 * 10**6, transcendentals=10**6),
    )(*args)


def shape(dims, kind):
    return jax.ShapeDtypeStruct(dims, kind)


def ordered(pieces, at):
    whole = jnp.zeros((4,) + pieces[0][1].shape, pieces[0][1].dtype)
    for offset, block in pieces:
        whole = lax.dynamic_update_slice(whole, block[None], (lax.rem(at + offset + 4, 4), 0, 0))
    return whole.reshape((-1,) + whole.shape[2:])


def gather_near(w, at):
    half = w.shape[0] // 2
    two = jnp.concatenate([shifted(w[:half], Z, 2), shifted(w[half:], Z, -2)], axis=0)
    return ordered([(0, w), (-1, shifted(w, Z, 1)), (1, shifted(w, Z, -1)), (2, two)], at)


def after(value, earlier):
    return lax.optimization_barrier((value, earlier))[0]


def on_device(
    hidden, steer, w_x, w_z, w_shared, conv_x, conv_shared, dt_bias, decay_rate, skip, norm_gain
):
    rows = hidden.shape[0]
    heads = dt_bias.shape[0]
    width = w_x.shape[1]
    ways = size_of(HEAD)
    maps = 2 * STATE // ways
    head_at = lax.axis_index(HEAD)
    seq_at = lax.axis_index(SEQ)
    x_at = lax.axis_index("x")
    z_at = lax.axis_index(Z)
    near_at = lax.axis_index("zl")

    halo = shifted(hidden[rows - HALO :], SEQ, 1, wrap=False)
    ext = jnp.concatenate([halo, hidden], axis=0)
    ext = (ext.astype(f32) + steer.astype(f32)).astype(bf16)
    k = hidden.shape[1]
    per = k // size_of(SEQ)
    turned = ext.reshape(-1, 4, 4, 4, per).transpose(0, 3, 2, 1, 4).reshape(-1, k)

    small = w_shared.shape[0]
    share = jnp.concatenate(
        [
            w_shared[:, : 2 * STATE].reshape(small, ways, maps),
            w_shared[:, 2 * STATE :].reshape(small, ways, heads),
        ],
        axis=2,
    ).transpose(1, 0, 2)
    share = lax.all_to_all(share, HEAD, 0, 0).reshape(ways * small, maps + heads)
    share = spread(share, "x").reshape(-1, share.shape[1])

    far = spread(jnp.concatenate([w_x, w_z], axis=1), "zh").reshape(-1, 2 * width)
    own = gather_near(after(far[:, :width], turned), near_at)
    side_z = spread(far[:, width:], "x").reshape(-1, width)
    left, right, beyond = (shifted(own, "x", d) for d in (1, -1, 2))
    own_z = gather_near(after(side_z, own), near_at)
    share = spread(after(share, own), Z).reshape(-1, share.shape[1])
    s_sum = dot(share, ext, ((0,), (1,)))

    early = (lax.broadcasted_iota(jnp.int32, (rows + HALO, 1), 0) < HALO) & (seq_at == 0)
    b_raw = jnp.where(early.reshape(1, -1), 0.0, s_sum[:maps]).astype(bf16).astype(f32)
    taps = lax.dynamic_slice_in_dim(conv_shared, head_at * maps, maps, 1).T
    b_conv = jnp.zeros((maps, rows), f32)
    for j in range(CONV):
        first = HALO - CONV + 1 + j
        b_conv = b_conv + b_raw[:, first : first + rows] * taps[:, j : j + 1]
    b_conv = jax.nn.silu(b_conv).astype(bf16)
    both = spread(b_conv, HEAD).reshape(2 * STATE, rows)

    def columns_of(offset):
        depth = own.shape[0]
        return lax.dynamic_slice_in_dim(turned, lax.rem(x_at + (offset + 4), 4) * depth, depth, 1)

    x_sum = dot(columns_of(0), own) + dot(columns_of(-1), left) + dot(columns_of(1), right)
    x_sum = x_sum + dot(columns_of(2), after(beyond, (both, own_z)))
    x_raw = jnp.where(early, 0.0, x_sum).astype(bf16)

    groups = width // STATE
    y, c_map, grown, ends = call(
        local_pass,
        (
            shape((rows, width), f32),
            shape((rows, STATE), bf16),
            shape((rows, width), f32),
            shape((groups, STATE + LOGS, STATE), bf16),
        ),
        x_raw,
        both,
        s_sum[maps:, HALO:],
        conv_x,
        dt_bias.reshape(-1, 1),
        decay_rate.reshape(-1, 1),
        jnp.repeat(skip, DIM).reshape(1, -1),
    )

    ends = lax.all_to_all(ends, "x", 0, 0)
    mine = call(group_pass, shape((STATE + LOGS, STATE), bf16), ends)
    totals = spread(mine, Z)
    starts = call(
        prefix_pass, shape((4, STATE, STATE), bf16), z_at.reshape(1), totals, ends, scalars=1
    )
    state_in = lax.all_to_all(starts, "x", 0, 0)

    turned_z = turned[HALO:].reshape(rows, 4, 4, -1).swapaxes(1, 2).reshape(rows, -1)
    z_raw = dot(turned_z, own_z).astype(bf16)
    gated, squares = call(
        gate_pass,
        (shape((rows, width), f32), shape((8, rows), f32)),
        y,
        c_map,
        grown,
        state_in,
        z_raw,
    )
    squares = jnp.sum(spread(squares[0].reshape(4, -1), HEAD), axis=0).reshape(rows)
    scale = lax.rsqrt(squares / (width * ways) + 1e-05)
    return (gated * scale[:, None] * norm_gain).astype(bf16)


def solution(mesh):
    mesh = Mesh(mesh.devices.reshape(tuple(SIZES.values())), tuple(SIZES))
    placed = (
        P(SEQ, None),
        P(),
        P(SEQ, HEAD),
        P(SEQ, HEAD),
        P(SEQ + HEAD, None),
        P(None, HEAD),
        P(),
        P(HEAD),
        P(HEAD),
        P(HEAD),
        P(HEAD),
    )
    return jax.shard_map(
        on_device, mesh=mesh, in_specs=placed, out_specs=P(SEQ, HEAD), check_vma=False
    )
```
